32 devices in a mesh: pack: 8 (over z, y), ctx: 4 (over x, core).
Axes of the slice: x: 2, y: 2, z: 4, core: 2. Of those that a mesh axis runs over, the one named last changes fastest.
Arguments:
- signals: bfloat16 [4096, 10240], P(('pack', 'ctx')), may hold values from -36 to 36
- state_io: bfloat16 [4096, 256], P(('pack', 'ctx')), may hold values from -0.8984375 to 0.8984375
- step_raw: bfloat16 [4096, 80], P(('pack', 'ctx')), may hold values from -4 to 4
- row_target: int32 [8, 4, 16], P('pack', 'ctx'), may hold values from 0 to 127, as said below
- table_start: int32 [8, 4], P('pack', 'ctx'), may hold values 0 or 1
- log_rate: float32 [80], replicated, may hold values from -11 to -2
- step_bias: float32 [80], replicated, may hold values from -0.5 to 0.5
- skip_gain: float32 [80], replicated, may hold values from 0.5 to 1.5
- norm_gain: float32 [5120], replicated, may hold values from 0.5 to 1.5
Outputs:
- gated: bfloat16 [4096, 5120], P(('pack', 'ctx'))
The draws below stay inside these ranges and needn't reach their ends.
Inputs may be any that keep to these rules, and one draw needn't show every extreme that they name: With t = row_target[p, c, j], t // 16 is the sequence that takes the row and t % 16 its row slot in slab c of that sequence; every slot of every slab is taken exactly once, and the rows of one device go exactly 2 to each sequence.
All inputs are finite; a program needn't handle non-finite values. No bound on the sum of `table_start` on one device may be relied on, other than what follows from the above.
Results may differ from the reference program's by a relative error of at most 0.0046.
Values may be sent and summed in bfloat16 or wider, within the bound.
A program may use at most 192 MiB of HBM per device.

```python
import math
from functools import partial
import jax
import jax.numpy as jnp
from jax import lax

HEADS = 80
HEAD_DIM = 64
STATE = 128
GROUP = 128
ROW = 8
CAP = 2
ROWS_DEV = 16
DI = 5120
SEQS = 8
SLABS = 4
SEQ_LEN = 512
GROUPS = 4
TOKENS = 4096


def draw_signals(key, part):
    key_cols, key_rows, key_vals = jax.random.split(key, 3)
    col_scale = jnp.exp(jax.random.uniform(key_cols, (2 * DI,), jnp.float32, math.log(0.3), math.log(3.0)))
    row_scale = jnp.exp(jax.random.uniform(key_rows, (TOKENS, 1), jnp.float32, math.log(0.3), math.log(3.0)))
    base_values = jnp.clip(jax.random.normal(key_vals, (TOKENS, 2 * DI), jnp.float32), -4.0, 4.0)
    return (base_values * col_scale[None, :] * row_scale).astype(jnp.bfloat16)


def draw_step_raw(key, part):
    key_offset, key_noise = jax.random.split(key, 2)
    offsets = jax.random.uniform(key_offset, (TOKENS // ROW, 1, 1), jnp.float32, -1.5, 1.0)
    noise_values = jnp.clip(0.6 * jax.random.normal(key_noise, (TOKENS // ROW, ROW, HEADS), jnp.float32), -2.4, 2.4)
    return (offsets + noise_values).reshape(TOKENS, HEADS).astype(jnp.bfloat16)


def draw_log_rate(key, part):
    key_pick, key_slow, key_fast = jax.random.split(key, 3)
    fast_share = 0.5
    fast_pick = jax.random.uniform(key_pick, (HEADS,), jnp.float32) < fast_share
    slow_log = jax.random.uniform(key_slow, (HEADS,), jnp.float32, math.log(0.1), 0.0) - jnp.log(jnp.float32(SEQ_LEN))
    fast_log = jax.random.uniform(key_fast, (HEADS,), jnp.float32, math.log(1.0 / 40.0), math.log(1.0 / 15.0))
    return jnp.where(fast_pick, fast_log, slow_log)


def seq_permutation(base_key, seq_index, length):
    return jax.random.permutation(jax.random.fold_in(base_key, seq_index), length)


def one_column(column_key):
    key_slot, key_shuffle = jax.random.split(column_key, 2)
    seq_ids = jnp.arange(SEQS, dtype=jnp.int32)
    slot_order = jax.vmap(partial(seq_permutation, key_slot, length=ROWS_DEV))(seq_ids)
    row_index = jnp.arange(ROWS_DEV, dtype=jnp.int32)
    destination = row_index // CAP
    within = row_index % CAP
    source_pos = seq_ids[:, None] * CAP + within[None, :]
    slot_taken = slot_order[destination[None, :], source_pos]
    target_value = destination[None, :] * ROWS_DEV + slot_taken
    shuffle = jax.vmap(partial(seq_permutation, key_shuffle, length=ROWS_DEV))(seq_ids)
    return jnp.take_along_axis(target_value, shuffle, axis=1)


def draw_row_target(key, part):
    column_keys = jax.vmap(partial(jax.random.fold_in, key))(jnp.arange(SLABS))
    columns = jax.vmap(one_column)(column_keys)
    return jnp.transpose(columns, (1, 0, 2)).astype(jnp.int32)


def plant(array, key, low, high):
    longest = array.shape.index(max(array.shape))
    spots = []
    for shift in (0, 1):
        where = [jax.random.randint(jax.random.fold_in(key, axis), (), 0, length) for axis, length in enumerate(array.shape)]
        where[longest] = (where[longest] + shift) % array.shape[longest]
        spots.append(tuple(where))
    return array.at[spots[0]].set(low).at[spots[1]].set(high)


def levels(stream_key, extent, cuts, low, largest):
    def one(axis_at, parts):
        steps = jax.random.uniform(jax.random.fold_in(jax.random.fold_in(stream_key, 6), axis_at), (parts,), jnp.float32, low / len(cuts), largest / len(cuts))
        return jnp.repeat(jnp.exp(steps), extent[axis_at] // parts).reshape((-1,) + (1,) * (len(extent) - axis_at - 1))

    gain = one(*cuts[0])
    for cut in cuts[1:]:
        gain = gain * one(*cut)
    return gain


def gaussian(own_key, shape, width, most, cuts=(), kind=jnp.bfloat16):
    array = width * jax.random.normal(own_key, shape, jnp.float32)
    if cuts:
        array = array * levels(own_key, shape, cuts, -0.22, 0.18)
    return jnp.clip(array, -most, most).astype(kind)


def setup_inputs(seed: int = 0) -> dict:
    splits = jax.random.split(jax.random.key(seed), 10)
    signals = draw_signals(jax.random.fold_in(splits[9], 71), 0)
    state_io = gaussian(splits[1], (TOKENS, 2 * STATE), 0.15, 0.8984375, ((0, 32),))
    step_raw = draw_step_raw(jax.random.fold_in(splits[9], 71), 0)
    row_target = draw_row_target(jax.random.fold_in(splits[9], 71), 0)
    table_start = plant((jax.random.randint(splits[4], (SEQS, GROUPS), 0, 5) < 1).astype(jnp.int32), jax.random.fold_in(splits[4], 1), 0, 1)
    log_rate = draw_log_rate(jax.random.fold_in(splits[9], 71), 0)
    step_bias = jnp.clip(jax.random.uniform(splits[6], (HEADS,), jnp.float32, -0.5, 0.5), -0.5, 0.5)
    skip_gain = jnp.clip(jax.random.uniform(splits[7], (HEADS,), jnp.float32, 0.5, 1.5), 0.5, 1.5)
    norm_gain = jnp.clip(1.0 + 0.1 * jax.random.normal(splits[8], (DI,), jnp.float32), 0.5, 1.5)
    return dict(signals=signals, state_io=state_io, step_raw=step_raw, row_target=row_target, table_start=table_start, log_rate=log_rate, step_bias=step_bias, skip_gain=skip_gain, norm_gain=norm_gain)


def group_step(state, inputs, log_rate, step_bias, skip_gain, norm_gain):
    signal_rows, io_rows, raw_rows, keep_flag = inputs
    gate_in = signal_rows[:, :DI]
    signal_in = signal_rows[:, DI:].reshape(GROUP, HEADS, HEAD_DIM)
    b_proj = io_rows[:, :STATE]
    c_proj = io_rows[:, STATE:]
    step_size = jax.nn.softplus(raw_rows.astype(jnp.float32) + step_bias)
    log_decay = -jnp.exp(log_rate) * step_size
    cumulative = jnp.cumsum(log_decay, axis=0)
    state = state * keep_flag
    c_dot_b = jnp.dot(c_proj, b_proj.T, preferred_element_type=jnp.float32)
    causal = jnp.arange(GROUP)[:, None] >= jnp.arange(GROUP)[None, :]
    per_head = cumulative.T
    log_gaps = per_head[:, :, None] - per_head[:, None, :]
    decay_mask = jnp.exp(jnp.where(causal[None], log_gaps, -jnp.inf))
    scores = (c_dot_b[None] * decay_mask * step_size.T[:, None, :]).astype(jnp.bfloat16)
    y_intra = jnp.einsum('hij,jhp->ihp', scores.astype(jnp.float32), signal_in.astype(jnp.float32))
    y_state = jnp.exp(cumulative)[:, :, None] * jnp.einsum('in,hpn->ihp', c_proj.astype(jnp.float32), state, precision=lax.Precision.HIGHEST)
    mixed = y_intra + y_state + skip_gain[None, :, None] * signal_in.astype(jnp.float32)
    to_end = jnp.exp(cumulative[-1][None, :] - cumulative) * step_size
    weighted = (signal_in.astype(jnp.float32) * to_end[:, :, None]).astype(jnp.bfloat16)
    new_state = jnp.exp(cumulative[-1])[:, None, None] * state + jnp.einsum('jhp,jn->hpn', weighted.astype(jnp.float32), b_proj.astype(jnp.float32))
    gated = mixed.reshape(GROUP, DI) * jax.nn.silu(gate_in.astype(jnp.float32))
    result = (gated * lax.rsqrt(lax.optimization_barrier(jnp.mean(gated * gated, axis=-1, keepdims=True)) + 1e-05) * norm_gain).astype(jnp.bfloat16)
    return (new_state, result)

def reference(signals, state_io, step_raw, row_target, table_start, log_rate, step_bias, skip_gain, norm_gain):
    row_total = SEQS * SLABS * ROWS_DEV
    targets = row_target.reshape(row_total).astype(jnp.int32)
    slab_of = (jnp.arange(row_total, dtype=jnp.int32) // ROWS_DEV % SLABS).astype(jnp.int32)
    placed_at = (targets // ROWS_DEV * (SLABS * ROWS_DEV) + slab_of * ROWS_DEV + targets % ROWS_DEV).astype(jnp.int32)
    source_of = jnp.zeros((row_total,), jnp.int32).at[placed_at].set(jnp.arange(row_total, dtype=jnp.int32))
    source_of = source_of.reshape(SEQS, SLABS * ROWS_DEV)
    signal_blocks = signals.reshape(row_total, ROW, 2 * DI)
    io_blocks = state_io.reshape(row_total, ROW, 2 * STATE)
    raw_blocks = step_raw.reshape(row_total, ROW, HEADS)
    keep_all = (1 - table_start).astype(jnp.float32)
    step_fn = partial(group_step, log_rate=log_rate, step_bias=step_bias, skip_gain=skip_gain, norm_gain=norm_gain)

    def one_sequence(packed):
        rows_used, keep_seq = packed

        def gather_rows(blocks):
            return jnp.take(blocks, rows_used, axis=0).reshape(GROUPS, GROUP, blocks.shape[-1])
        inputs = (gather_rows(signal_blocks), gather_rows(io_blocks), gather_rows(raw_blocks), keep_seq)
        zero_state = jnp.zeros((HEADS, HEAD_DIM, STATE), jnp.float32)
        final_state, outputs = lax.scan(step_fn, zero_state, inputs)
        return outputs.reshape(SEQ_LEN, DI)
    result = lax.map(one_sequence, (source_of, keep_all))
    return result.reshape(TOKENS, DI)
```

```python
import functools

import jax
import jax.numpy as jnp
from jax import lax
from jax.experimental import pallas as pl
from jax.experimental.pallas import tpu as pltpu
from jax.sharding import PartitionSpec as P

GROUP = 128
ROW = 8
CHUNK = 512
GATE_AFTER = True
MESH = pl.DeviceIdType.MESH


def passed_along(block, axis, distance):
    devices = range(lax.axis_size(axis))
    route = [(i - distance, i) for i in devices if i - distance in devices]
    return lax.ppermute(block, axis, route)


def body(
    signals, state_io, step_raw, row_target, table_start, log_rate, step_bias, skip_gain, norm_gain
):
    pack_size = lax.axis_size("pack")
    ctx_size = lax.axis_size("ctx")
    row_count = row_target.shape[2]
    capacity = row_count // pack_size
    slot_count = pack_size * capacity
    inner_width = signals.shape[1] // 2
    head_count = log_rate.shape[0]
    head_width = inner_width // head_count
    state_width = state_io.shape[1] // 2
    token_count = row_count * ROW
    groups = token_count // GROUP
    targets = row_target.reshape(row_count)
    destination = targets // row_count
    row_index = jnp.arange(row_count, dtype=jnp.int32)
    earlier_rows = (destination[:, None] == destination[None, :]) & (
        row_index[None, :] < row_index[:, None]
    )
    earlier_count = jnp.sum(earlier_rows.astype(jnp.int32), axis=1)
    position = destination * capacity + earlier_count
    send_match = position[None, :] == jnp.arange(slot_count, dtype=jnp.int32)[:, None]
    filled = jnp.any(send_match, axis=1)
    source_row = jnp.where(
        filled, jnp.sum(jnp.where(send_match, row_index[None, :], 0), axis=1), row_count
    )
    send_slot = jnp.where(
        filled, jnp.sum(jnp.where(send_match, (targets % row_count)[None, :], 0), axis=1), -1
    )

    def outgoing(values):
        blocks = values.reshape(row_count, ROW, values.shape[1])
        return jnp.take(blocks, source_row, axis=0, mode="fill", fill_value=0)

    signal_got, io_got, raw_got, slot_got = (
        lax.all_to_all(
            outgoing(signals[:, inner_width:]), "pack", split_axis=0, concat_axis=0, tiled=True
        ),
        lax.all_to_all(outgoing(state_io), "pack", split_axis=0, concat_axis=0, tiled=True),
        lax.all_to_all(outgoing(step_raw), "pack", split_axis=0, concat_axis=0, tiled=True),
        lax.all_to_all(send_slot, "pack", split_axis=0, concat_axis=0, tiled=True),
    )
    slot_match = slot_got[None, :] == row_index[:, None]
    source_of = jnp.sum(
        jnp.where(slot_match, jnp.arange(slot_count, dtype=jnp.int32)[None, :], 0), axis=1
    )

    def arrange(values):
        return jnp.take(values, source_of, axis=0).reshape(token_count, values.shape[-1])

    signal_in = arrange(signal_got)
    io_rows = arrange(io_got)
    raw_rows = arrange(raw_got)
    inputs = signal_in.reshape(groups, GROUP, head_count, head_width)
    b_proj = io_rows[:, :state_width].reshape(groups, GROUP, state_width)
    c_proj = io_rows[:, state_width:].reshape(groups, GROUP, state_width)
    step_size = jax.nn.softplus(raw_rows.astype(jnp.float32) + step_bias).reshape(
        groups, GROUP, head_count
    )
    log_decay = -jnp.exp(log_rate) * step_size
    cumulative = jnp.cumsum(log_decay, axis=1)
    c_dot_b = jnp.einsum("kin,kjn->kij", c_proj, b_proj, preferred_element_type=jnp.float32)
    causal = jnp.arange(GROUP)[:, None] >= jnp.arange(GROUP)[None, :]
    per_head = cumulative.transpose(0, 2, 1)
    log_gaps = per_head[:, :, :, None] - per_head[:, :, None, :]
    decay_mask = jnp.exp(jnp.where(causal[None, None], log_gaps, -jnp.inf))
    scores = (c_dot_b[:, None] * decay_mask * step_size.transpose(0, 2, 1)[:, :, None, :]).astype(
        jnp.bfloat16
    )
    y_intra = jnp.einsum("khij,kjhp->kihp", scores, inputs, preferred_element_type=jnp.float32)
    to_end = jnp.exp(cumulative[:, -1:, :] - cumulative) * step_size
    weighted = (inputs.astype(jnp.float32) * to_end[..., None]).astype(jnp.bfloat16)
    local_state = jnp.einsum("kjhp,kjn->khpn", weighted, b_proj, preferred_element_type=jnp.float32)
    keep_flag = (1 - table_start.reshape(groups)).astype(jnp.float32)
    group_decay = jnp.exp(cumulative[:, -1, :])
    carry_gain = []
    carry_base = []
    gain_now = keep_flag[0] * jnp.ones((head_count,), jnp.float32)
    base_now = jnp.zeros((head_count, head_width, state_width), jnp.float32)
    for group_id in range(groups):
        if group_id > 0:
            gain_now = keep_flag[group_id] * (group_decay[group_id - 1] * gain_now)
            base_now = keep_flag[group_id] * (
                group_decay[group_id - 1][:, None, None] * base_now + local_state[group_id - 1]
            )
        carry_gain.append(gain_now)
        carry_base.append(base_now)
    leave_gain = group_decay[-1] * gain_now
    leave_base = group_decay[-1][:, None, None] * base_now + local_state[-1]
    incoming = jnp.zeros((head_count, head_width, state_width), jnp.float32)
    for hop_index in range(ctx_size - 1):
        incoming = passed_along(leave_gain[:, None, None] * incoming + leave_base, "ctx", 1)
    entering = jnp.stack(carry_gain)[:, :, None, None] * incoming[None] + jnp.stack(carry_base)
    y_state = jnp.exp(cumulative)[..., None] * jnp.einsum(
        "kin,khpn->kihp", c_proj.astype(jnp.float32), entering, precision=lax.Precision.HIGHEST
    )
    mixed = y_intra + y_state + skip_gain[None, None, :, None] * inputs.astype(jnp.float32)
    mixed = mixed.reshape(token_count, inner_width)
    gate_got = lax.all_to_all(
        outgoing(signals[:, :inner_width]), "pack", split_axis=0, concat_axis=0, tiled=True
    )
    gate_in = arrange(gate_got)
    gated = mixed * jax.nn.silu(gate_in.astype(jnp.float32))
    result = gated * lax.rsqrt(jnp.mean(gated * gated, axis=-1, keepdims=True) + 1e-05) * norm_gain
    return result.astype(jnp.bfloat16)


def exact_permute(onehot, values):
    return jnp.dot(onehot, values, preferred_element_type=jnp.float32).astype(jnp.bfloat16)


def split_sum(values):
    high = values.astype(jnp.bfloat16)
    low = (values - high.astype(jnp.float32)).astype(jnp.bfloat16)
    return jnp.concatenate([high, low], axis=1)


def fused_kernel(
    pack_size,
    ctx_size,
    head_width,
    signals,
    state_io,
    step_raw,
    row_target,
    table_start,
    log_rate,
    step_bias,
    skip_gain,
    norm_gain,
    out,
    order,
    pieces,
    small,
    x_stage,
    z_stage,
    x_got,
    z_got,
    heads,
    mixed,
    grow,
    local,
    leave,
    enter,
    x_send,
    x_recv,
    z_send,
    z_recv,
    s_send,
    s_recv,
):
    tokens = GROUP
    rows = tokens // ROW
    inner = norm_gain.shape[1]
    head_count = log_rate.shape[1]
    width = state_io.shape[1]
    state = width // 2
    block = tokens // pack_size
    chunk = CHUNK
    chunks = inner // chunk
    me = lax.axis_index("pack")
    slab = lax.axis_index("ctx")
    barrier = pltpu.get_barrier_semaphore()
    for off in range(1, pack_size):
        pl.semaphore_signal(
            barrier, inc=1, device_id={"pack": lax.rem(me + off, pack_size)}, device_id_type=MESH
        )
    for off in range(1, ctx_size):
        pl.semaphore_signal(
            barrier, inc=1, device_id={"ctx": lax.rem(slab + off, ctx_size)}, device_id_type=MESH
        )

    lane = lax.broadcasted_iota(jnp.int32, (tokens, tokens), 1)
    sub = lax.broadcasted_iota(jnp.int32, (tokens, tokens), 0)
    goal_lane = jnp.zeros((1, tokens), jnp.int32)
    goal_rows = []
    slot_rows = []
    for j in range(rows):
        target = row_target[j]
        goal = target // rows
        goal_lane = jnp.where(lane[:1] // ROW == j, goal, goal_lane)
        goal_rows.append(jnp.full((ROW, tokens), goal, jnp.int32))
        slot_rows.append(jnp.full((ROW, tokens), target - goal * rows, jnp.int32))
    goal_sub = jnp.concatenate(goal_rows, axis=0)
    slot_sub = jnp.concatenate(slot_rows, axis=0)
    earlier = (goal_sub == goal_lane) & (sub // ROW < lane // ROW) & (sub % ROW == 0)
    earlier = jnp.sum(jnp.where(earlier, 1.0, 0.0), axis=0, keepdims=True).astype(jnp.int32)
    place = (goal_lane * (rows // pack_size) + earlier) * ROW + lane[:1] % ROW
    send_order = jnp.where(sub == place, 1.0, 0.0).astype(jnp.bfloat16)
    small[:, :width] = state_io[...]
    small[:, width : width + 128] = jnp.zeros((tokens, 128), jnp.bfloat16)
    small[:, width : width + head_count] = step_raw[...]
    small[:, width + 128 :] = (slot_sub * ROW + sub % ROW).astype(jnp.float32).astype(jnp.bfloat16)
    x_stage[:, :, inner:] = exact_permute(send_order, small[...]).reshape(
        pack_size, block, width + 256
    )

    @pl.loop(0, chunks)
    def _(c):
        at = pl.multiple_of(c * chunk, chunk)
        x_stage[:, :, pl.ds(at, chunk)] = exact_permute(
            send_order, signals[:, pl.ds(inner + at, chunk)]
        ).reshape(pack_size, block, chunk)

    pl.semaphore_wait(barrier, pack_size + ctx_size - 2)

    def x_copy(peer, slot):
        return pltpu.make_async_remote_copy(
            src_ref=x_stage.at[peer],
            dst_ref=x_got.at[slot],
            send_sem=x_send.at[peer],
            recv_sem=x_recv.at[slot],
            device_id={"pack": peer},
            device_id_type=MESH,
        )

    def z_copy(peer, slot):
        return pltpu.make_async_remote_copy(
            src_ref=z_stage.at[peer],
            dst_ref=z_got.at[slot],
            send_sem=z_send.at[peer],
            recv_sem=z_recv.at[slot],
            device_id={"pack": peer},
            device_id_type=MESH,
        )

    def s_copy(c):
        return pltpu.make_async_remote_copy(
            src_ref=leave.at[c],
            dst_ref=enter.at[c],
            send_sem=s_send.at[c],
            recv_sem=s_recv.at[c],
            device_id={"ctx": lax.rem(slab + 1, ctx_size)},
            device_id_type=MESH,
        )

    for off in range(1, pack_size):
        x_copy(lax.rem(me + off, pack_size), me).start()

    @pl.loop(0, chunks)
    def _(c):
        at = pl.multiple_of(c * chunk, chunk)
        z_stage[:, :, pl.ds(at, chunk)] = exact_permute(
            send_order, signals[:, pl.ds(at, chunk)]
        ).reshape(pack_size, block, chunk)

    x_got[me] = x_stage[me]
    z_got[me] = z_stage[me]
    if GATE_AFTER:
        for off in range(1, pack_size):
            x_copy(lax.rem(me + off, pack_size), me).wait_send()
    for off in range(1, pack_size):
        z_copy(lax.rem(me + off, pack_size), me).start()
    for off in range(1, pack_size):
        peer = lax.rem(me + off, pack_size)
        x_copy(peer, peer).wait_recv()

    heads[...] = jnp.zeros(heads.shape, jnp.float32)
    heads[0:1, :head_count] = log_rate[...]
    heads[1:2, :head_count] = step_bias[...]
    heads[2:3, :head_count] = skip_gain[...]
    maps = x_got[:, :, inner : inner + width].reshape(tokens, width)
    b_map = maps[:, :state]
    c_map = maps[:, state:]
    raw = x_got[:, :, inner + width : inner + width + 128].reshape(tokens, 128)
    spot = x_got[:, :, inner + width + 128 :].reshape(tokens, 128).astype(jnp.float32)
    spot_lane = spot.T
    past = spot_lane <= spot
    order[...] = jnp.where(spot_lane == sub.astype(jnp.float32), 1.0, 0.0).astype(jnp.bfloat16)
    u = raw.astype(jnp.float32) + heads[1:2, :]
    dt = jnp.maximum(u, 0.0) + jnp.log(1.0 + jnp.exp(-jnp.abs(u)))
    a = -jnp.exp(heads[0:1, :]) * dt
    cum = jnp.dot(
        jnp.where(past, 1.0, 0.0),
        a,
        preferred_element_type=jnp.float32,
        precision=lax.Precision.HIGHEST,
    )
    last = jnp.sum(a, axis=0, keepdims=True)
    mid = 0.5 * last
    dots = lax.dot_general(
        c_map, b_map, (((1,), (1,)), ((), ())), preferred_element_type=jnp.float32
    )
    dots = jnp.where(past, dots, 0.0).astype(jnp.bfloat16)
    b_flip = b_map.astype(jnp.float32).T.astype(jnp.bfloat16)
    left = jnp.concatenate([dots, b_flip], axis=0)
    shrink = split_sum(jnp.exp(mid - cum) * dt)
    rise = split_sum(jnp.exp(cum - mid))
    keep = (1 - table_start[0]).astype(jnp.float32)
    half = jnp.exp(mid)
    vectors = split_sum(
        jnp.concatenate(
            [half, keep * half, keep * (half * half), heads[2:3, :], jnp.zeros((4, 128), jnp.float32)],
            axis=0,
        )
    )
    pieces[0:tokens] = shrink
    pieces[tokens : 2 * tokens] = rise
    pieces[2 * tokens : 2 * tokens + 8] = vectors
    pieces[2 * tokens + 8 :] = jnp.zeros((8, 256), jnp.bfloat16)

    def spread(c, part):
        head = lax.broadcasted_iota(jnp.int32, (256, chunk), 0) % 128
        column = lax.broadcasted_iota(jnp.int32, (256, chunk), 1) // head_width
        pick = jnp.where(head == column + c * (chunk // head_width), 1.0, 0.0)
        return jnp.dot(part, pick.astype(jnp.bfloat16), preferred_element_type=jnp.float32)

    @pl.loop(0, chunks)
    def _(c):
        at = pl.multiple_of(c * chunk, chunk)
        wide = spread(c, pieces[...])
        ups = wide[tokens : 2 * tokens]
        half_wide = wide[2 * tokens : 2 * tokens + 1]
        x = x_got[:, :, pl.ds(at, chunk)].reshape(tokens, chunk).astype(jnp.float32)
        scaled = (x * wide[:tokens]).astype(jnp.bfloat16)
        both = jnp.dot(left, scaled, preferred_element_type=jnp.float32)
        y = both[:tokens] * ups + wide[2 * tokens + 3 : 2 * tokens + 4] * x
        mixed[:, :, pl.ds(at, chunk)] = y.reshape(pack_size, block, chunk)
        leaving = both[tokens:] * half_wide

        @pl.when(slab == 0)
        def _():
            leave[c] = leaving.astype(jnp.bfloat16)
            s_copy(c).start()

        @pl.when(slab > 0)
        def _():
            local[c] = leaving
            grow[c] = ups * wide[2 * tokens + 1 : 2 * tokens + 2]

    @pl.when(slab > 0)
    def _():
        @pl.loop(0, chunks)
        def _(c):
            at = pl.multiple_of(c * chunk, chunk)
            decay = spread(c, pieces[2 * tokens :])[2:3]
            s_copy(c).wait_recv()
            got = enter[c]

            @pl.when(slab < ctx_size - 1)
            def _():
                leave[c] = (decay * got.astype(jnp.float32) + local[c]).astype(jnp.bfloat16)
                s_copy(c).start()

            carried = jnp.dot(c_map, got, preferred_element_type=jnp.float32) * grow[c]
            mixed[:, :, pl.ds(at, chunk)] += carried.reshape(pack_size, block, chunk)

    for off in range(pack_size):
        peer = lax.rem(me + off, pack_size)
        if off > 0:
            z_copy(peer, peer).wait_recv()
        z = z_got[peer].astype(jnp.float32)
        g = mixed[peer] * (z / (1.0 + jnp.exp(-z)))
        scale = lax.rsqrt(jnp.mean(g * g, axis=-1, keepdims=True) + 1e-05)
        out[peer] = (g * scale * norm_gain[...]).astype(jnp.bfloat16)

    for off in range(1, pack_size):
        peer = lax.rem(me + off, pack_size)
        if not GATE_AFTER:
            x_copy(peer, me).wait_send()
        z_copy(peer, me).wait_send()

    @pl.when(slab < ctx_size - 1)
    def _():
        @pl.loop(0, chunks)
        def _(c):
            s_copy(c).wait_send()


def fused_body(
    signals, state_io, step_raw, row_target, table_start, log_rate, step_bias, skip_gain, norm_gain
):
    pack_size = lax.axis_size("pack")
    ctx_size = lax.axis_size("ctx")
    tokens = signals.shape[0]
    inner = signals.shape[1] // 2
    width = state_io.shape[1]
    state = width // 2
    head_count = log_rate.shape[0]
    block = tokens // pack_size
    chunks = inner // CHUNK
    vmem = pl.BlockSpec(memory_space=pltpu.VMEM)
    smem = pl.BlockSpec(memory_space=pltpu.SMEM)
    unsorted, order = pl.pallas_call(
        functools.partial(fused_kernel, pack_size, ctx_size, inner // head_count),
        out_shape=(
            jax.ShapeDtypeStruct((pack_size, block, inner), jnp.bfloat16),
            jax.ShapeDtypeStruct((tokens, tokens), jnp.bfloat16),
        ),
        in_specs=[vmem, vmem, vmem, smem, smem, vmem, vmem, vmem, vmem],
        out_specs=(vmem, vmem),
        scratch_shapes=[
            pltpu.VMEM((2 * tokens + 16, 256), jnp.bfloat16),
            pltpu.VMEM((tokens, width + 256), jnp.bfloat16),
            pltpu.VMEM((pack_size, block, inner + width + 256), jnp.bfloat16),
            pltpu.VMEM((pack_size, block, inner), jnp.bfloat16),
            pltpu.VMEM((pack_size, block, inner + width + 256), jnp.bfloat16),
            pltpu.VMEM((pack_size, block, inner), jnp.bfloat16),
            pltpu.VMEM((8, 128), jnp.float32),
            pltpu.VMEM((pack_size, block, inner), jnp.float32),
            pltpu.VMEM((chunks, tokens, CHUNK), jnp.float32),
            pltpu.VMEM((chunks, state, CHUNK), jnp.float32),
            pltpu.VMEM((chunks, state, CHUNK), jnp.bfloat16),
            pltpu.VMEM((chunks, state, CHUNK), jnp.bfloat16),
            pltpu.SemaphoreType.DMA((pack_size,)),
            pltpu.SemaphoreType.DMA((pack_size,)),
            pltpu.SemaphoreType.DMA((pack_size,)),
            pltpu.SemaphoreType.DMA((pack_size,)),
            pltpu.SemaphoreType.DMA((chunks,)),
            pltpu.SemaphoreType.DMA((chunks,)),
        ],
        compiler_params=pltpu.CompilerParams(
            collective_id=0, has_side_effects=True, vmem_limit_bytes=48 * 1024 * 1024
        ),
    )(
        signals,
        state_io,
        step_raw,
        row_target.reshape(-1),
        table_start.reshape(-1),
        log_rate.reshape(1, -1),
        step_bias.reshape(1, -1),
        skip_gain.reshape(1, -1),
        norm_gain.reshape(1, -1),
    )
    return exact_permute(order, unsorted.reshape(tokens, inner))


def either_body(*arguments):
    one_group = arguments[0].shape[0] == GROUP and arguments[0].shape[1] % (2 * CHUNK) == 0
    return (fused_body if one_group else body)(*arguments)


def solution(mesh):
    return jax.shard_map(
        either_body,
        mesh=mesh,
        in_specs=(
            P(("pack", "ctx"), None),
            P(("pack", "ctx"), None),
            P(("pack", "ctx"), None),
            P("pack", "ctx", None),
            P("pack", "ctx"),
            P(),
            P(),
            P(),
            P(),
        ),
        out_specs=P(("pack", "ctx"), None),
        check_vma=False,
    )
```

```python
import functools

import jax
import jax.numpy as jnp
from jax import lax
from jax.experimental import pallas as pl
from jax.experimental.pallas import tpu as pltpu
from jax.sharding import PartitionSpec as P

GROUP = 128
ROW = 8
CHUNK = 512
GATE_AFTER = True
MESH = pl.DeviceIdType.MESH


def passed_along(block, axis, distance):
    devices = range(lax.axis_size(axis))
    route = [(i - distance, i) for i in devices if i - distance in devices]
    return lax.ppermute(block, axis, route)


def body(
    signals, state_io, step_raw, row_target, table_start, log_rate, step_bias, skip_gain, norm_gain
):
    pack_size = lax.axis_size("pack")
    ctx_size = lax.axis_size("ctx")
    row_count = row_target.shape[2]
    capacity = row_count // pack_size
    slot_count = pack_size * capacity
    inner_width = signals.shape[1] // 2
    head_count = log_rate.shape[0]
    head_width = inner_width // head_count
    state_width = state_io.shape[1] // 2
    token_count = row_count * ROW
    groups = token_count // GROUP
    targets = row_target.reshape(row_count)
    destination = targets // row_count
    row_index = jnp.arange(row_count, dtype=jnp.int32)
    earlier_rows = (destination[:, None] == destination[None, :]) & (
        row_index[None, :] < row_index[:, None]
    )
    earlier_count = jnp.sum(earlier_rows.astype(jnp.int32), axis=1)
    position = destination * capacity + earlier_count
    send_match = position[None, :] == jnp.arange(slot_count, dtype=jnp.int32)[:, None]
    filled = jnp.any(send_match, axis=1)
    source_row = jnp.where(
        filled, jnp.sum(jnp.where(send_match, row_index[None, :], 0), axis=1), row_count
    )
    send_slot = jnp.where(
        filled, jnp.sum(jnp.where(send_match, (targets % row_count)[None, :], 0), axis=1), -1
    )

    def outgoing(values):
        blocks = values.reshape(row_count, ROW, values.shape[1])
        return jnp.take(blocks, source_row, axis=0, mode="fill", fill_value=0)

    signal_got, io_got, raw_got, slot_got = (
        lax.all_to_all(
            outgoing(signals[:, inner_width:]), "pack", split_axis=0, concat_axis=0, tiled=True
        ),
        lax.all_to_all(outgoing(state_io), "pack", split_axis=0, concat_axis=0, tiled=True),
        lax.all_to_all(outgoing(step_raw), "pack", split_axis=0, concat_axis=0, tiled=True),
        lax.all_to_all(send_slot, "pack", split_axis=0, concat_axis=0, tiled=True),
    )
    slot_match = slot_got[None, :] == row_index[:, None]
    source_of = jnp.sum(
        jnp.where(slot_match, jnp.arange(slot_count, dtype=jnp.int32)[None, :], 0), axis=1
    )

    def arrange(values):
        return jnp.take(values, source_of, axis=0).reshape(token_count, values.shape[-1])

    signal_in = arrange(signal_got)
    io_rows = arrange(io_got)
    raw_rows = arrange(raw_got)
    inputs = signal_in.reshape(groups, GROUP, head_count, head_width)
    b_proj = io_rows[:, :state_width].reshape(groups, GROUP, state_width)
    c_proj = io_rows[:, state_width:].reshape(groups, GROUP, state_width)
    step_size = jax.nn.softplus(raw_rows.astype(jnp.float32) + step_bias).reshape(
        groups, GROUP, head_count
    )
    log_decay = -jnp.exp(log_rate) * step_size
    cumulative = jnp.cumsum(log_decay, axis=1)
    c_dot_b = jnp.einsum("kin,kjn->kij", c_proj, b_proj, preferred_element_type=jnp.float32)
    causal = jnp.arange(GROUP)[:, None] >= jnp.arange(GROUP)[None, :]
    per_head = cumulative.transpose(0, 2, 1)
    log_gaps = per_head[:, :, :, None] - per_head[:, :, None, :]
    decay_mask = jnp.exp(jnp.where(causal[None, None], log_gaps, -jnp.inf))
    scores = (c_dot_b[:, None] * decay_mask * step_size.transpose(0, 2, 1)[:, :, None, :]).astype(
        jnp.bfloat16
    )
    y_intra = jnp.einsum("khij,kjhp->kihp", scores, inputs, preferred_element_type=jnp.float32)
    to_end = jnp.exp(cumulative[:, -1:, :] - cumulative) * step_size
    weighted = (inputs.astype(jnp.float32) * to_end[..., None]).astype(jnp.bfloat16)
    local_state = jnp.einsum("kjhp,kjn->khpn", weighted, b_proj, preferred_element_type=jnp.float32)
    keep_flag = (1 - table_start.reshape(groups)).astype(jnp.float32)
    group_decay = jnp.exp(cumulative[:, -1, :])
    carry_gain = []
    carry_base = []
    gain_now = keep_flag[0] * jnp.ones((head_count,), jnp.float32)
    base_now = jnp.zeros((head_count, head_width, state_width), jnp.float32)
    for group_id in range(groups):
        if group_id > 0:
            gain_now = keep_flag[group_id] * (group_decay[group_id - 1] * gain_now)
            base_now = keep_flag[group_id] * (
                group_decay[group_id - 1][:, None, None] * base_now + local_state[group_id - 1]
            )
        carry_gain.append(gain_now)
        carry_base.append(base_now)
    leave_gain = group_decay[-1] * gain_now
    leave_base = group_decay[-1][:, None, None] * base_now + local_state[-1]
    incoming = jnp.zeros((head_count, head_width, state_width), jnp.float32)
    for hop_index in range(ctx_size - 1):
        incoming = passed_along(leave_gain[:, None, None] * incoming + leave_base, "ctx", 1)
    entering = jnp.stack(carry_gain)[:, :, None, None] * incoming[None] + jnp.stack(carry_base)
    y_state = jnp.exp(cumulative)[..., None] * jnp.einsum(
        "kin,khpn->kihp", c_proj.astype(jnp.float32), entering, precision=lax.Precision.HIGHEST
    )
    mixed = y_intra + y_state + skip_gain[None, None, :, None] * inputs.astype(jnp.float32)
    mixed = mixed.reshape(token_count, inner_width)
    gate_got = lax.all_to_all(
        outgoing(signals[:, :inner_width]), "pack", split_axis=0, concat_axis=0, tiled=True
    )
    gate_in = arrange(gate_got)
    gated = mixed * jax.nn.silu(gate_in.astype(jnp.float32))
    result = gated * lax.rsqrt(jnp.mean(gated * gated, axis=-1, keepdims=True) + 1e-05) * norm_gain
    return result.astype(jnp.bfloat16)


def exact_permute(onehot, values):
    return jnp.dot(onehot, values, preferred_element_type=jnp.float32).astype(jnp.bfloat16)


def split_sum(values):
    high = values.astype(jnp.bfloat16)
    low = (values - high.astype(jnp.float32)).astype(jnp.bfloat16)
    return jnp.concatenate([high, low], axis=1)


def fused_kernel(
    pack_size,
    ctx_size,
    head_width,
    signals_hbm,
    state_io_hbm,
    step_flip_hbm,
    row_target_hbm,
    table_start_hbm,
    log_rate_hbm,
    step_bias_hbm,
    skip_gain_hbm,
    norm_gain_hbm,
    out,
    order,
    x_in,
    z_in,
    state_io,
    step_flip,
    row_target,
    table_start,
    log_rate,
    step_bias,
    skip_gain,
    norm_gain,
    pieces,
    spacing,
    small,
    x_stage,
    z_stage,
    x_got,
    z_got,
    heads,
    mixed,
    leave,
    enter,
    load,
    x_send,
    x_recv,
    z_send,
    z_recv,
    s_send,
    s_recv,
):
    tokens = GROUP
    rows = tokens // ROW
    inner = norm_gain.shape[1]
    head_count = log_rate.shape[1]
    width = state_io.shape[1]
    state = width // 2
    block = tokens // pack_size
    chunk = CHUNK
    chunks = inner // chunk
    me = lax.axis_index("pack")
    slab = lax.axis_index("ctx")
    loads = [
        pltpu.make_async_copy(source, held, load.at[i])
        for i, (source, held) in enumerate(
            (
                (row_target_hbm, row_target),
                (signals_hbm.at[:, pl.ds(inner, inner)], x_in),
                (state_io_hbm, state_io),
                (step_flip_hbm, step_flip),
                (signals_hbm.at[:, pl.ds(0, inner)], z_in),
                (table_start_hbm, table_start),
                (log_rate_hbm, log_rate),
                (step_bias_hbm, step_bias),
                (skip_gain_hbm, skip_gain),
                (norm_gain_hbm, norm_gain),
            )
        )
    ]
    for copy in loads:
        copy.start()
    barrier = pltpu.get_barrier_semaphore()
    for off in range(1, pack_size):
        pl.semaphore_signal(
            barrier, inc=1, device_id={"pack": lax.rem(me + off, pack_size)}, device_id_type=MESH
        )
    for off in range(1, ctx_size):
        pl.semaphore_signal(
            barrier, inc=1, device_id={"ctx": lax.rem(slab + off, ctx_size)}, device_id_type=MESH
        )

    lane = lax.broadcasted_iota(jnp.int32, (tokens, tokens), 1)
    sub = lax.broadcasted_iota(jnp.int32, (tokens, tokens), 0)
    head = lax.broadcasted_iota(jnp.int32, (256, chunk), 0) % 128
    column = lax.broadcasted_iota(jnp.int32, (256, chunk), 1) // head_width
    spacing[...] = head - column
    loads[0].wait()
    goal_lane = jnp.zeros((1, tokens), jnp.int32)
    goal_rows = []
    slot_rows = []
    for j in range(rows):
        target = row_target[j]
        goal = target // rows
        goal_lane = jnp.where(lane[:1] // ROW == j, goal, goal_lane)
        goal_rows.append(jnp.full((ROW, tokens), goal, jnp.int32))
        slot_rows.append(jnp.full((ROW, tokens), target - goal * rows, jnp.int32))
    goal_sub = jnp.concatenate(goal_rows, axis=0)
    slot_sub = jnp.concatenate(slot_rows, axis=0)
    earlier = (goal_sub == goal_lane) & (sub // ROW < lane // ROW) & (sub % ROW == 0)
    earlier = jnp.sum(jnp.where(earlier, 1.0, 0.0), axis=0, keepdims=True).astype(jnp.int32)
    place = (goal_lane * (rows // pack_size) + earlier) * ROW + lane[:1] % ROW
    send_order = jnp.where(sub == place, 1.0, 0.0).astype(jnp.bfloat16)
    for copy in loads[1:4]:
        copy.wait()
    small[:, :width] = state_io[...]
    heads[...] = jnp.zeros(heads.shape, jnp.float32)
    heads[:head_count] = step_flip[...].astype(jnp.float32)
    small[:, width : width + 128] = heads[...].T.astype(jnp.bfloat16)
    small[:, width + 128 :] = (slot_sub * ROW + sub % ROW).astype(jnp.float32).astype(jnp.bfloat16)
    x_stage[:, :, inner:] = exact_permute(send_order, small[...]).reshape(
        pack_size, block, width + 256
    )

    @pl.loop(0, chunks)
    def _(c):
        at = pl.multiple_of(c * chunk, chunk)
        x_stage[:, :, pl.ds(at, chunk)] = exact_permute(
            send_order, x_in[:, pl.ds(at, chunk)]
        ).reshape(pack_size, block, chunk)

    pl.semaphore_wait(barrier, pack_size + ctx_size - 2)

    def x_copy(peer, slot):
        return pltpu.make_async_remote_copy(
            src_ref=x_stage.at[peer],
            dst_ref=x_got.at[slot],
            send_sem=x_send.at[peer],
            recv_sem=x_recv.at[slot],
            device_id={"pack": peer},
            device_id_type=MESH,
        )

    def z_copy(peer, slot):
        return pltpu.make_async_remote_copy(
            src_ref=z_stage.at[peer],
            dst_ref=z_got.at[slot],
            send_sem=z_send.at[peer],
            recv_sem=z_recv.at[slot],
            device_id={"pack": peer},
            device_id_type=MESH,
        )

    def s_copy(c):
        return pltpu.make_async_remote_copy(
            src_ref=leave.at[c],
            dst_ref=enter.at[c],
            send_sem=s_send.at[c],
            recv_sem=s_recv.at[c],
            device_id={"ctx": lax.rem(slab + 1, ctx_size)},
            device_id_type=MESH,
        )

    for off in range(1, pack_size):
        x_copy(lax.rem(me + off, pack_size), me).start()

    for copy in loads[4:]:
        copy.wait()

    @pl.loop(0, chunks)
    def _(c):
        at = pl.multiple_of(c * chunk, chunk)
        z_stage[:, :, pl.ds(at, chunk)] = exact_permute(
            send_order, z_in[:, pl.ds(at, chunk)]
        ).reshape(pack_size, block, chunk)

    x_got[me] = x_stage[me]
    z_got[me] = z_stage[me]
    if GATE_AFTER:
        for off in range(1, pack_size):
            x_copy(lax.rem(me + off, pack_size), me).wait_send()
    for off in range(1, pack_size):
        z_copy(lax.rem(me + off, pack_size), me).start()
    for off in range(1, pack_size):
        peer = lax.rem(me + off, pack_size)
        x_copy(peer, peer).wait_recv()

    heads[0:8] = jnp.zeros((8, 128), jnp.float32)
    heads[0:1, :head_count] = log_rate[...]
    heads[1:2, :head_count] = step_bias[...]
    heads[2:3, :head_count] = skip_gain[...]
    maps = x_got[:, :, inner : inner + width].reshape(tokens, width)
    b_map = maps[:, :state]
    c_map = maps[:, state:]
    raw = x_got[:, :, inner + width : inner + width + 128].reshape(tokens, 128)
    spot = x_got[:, :, inner + width + 128 :].reshape(tokens, 128).astype(jnp.float32)
    spot_lane = spot.T
    past = spot_lane <= spot
    order[...] = jnp.where(spot_lane == sub.astype(jnp.float32), 1.0, 0.0).astype(jnp.bfloat16)
    u = raw.astype(jnp.float32) + heads[1:2, :]
    dt = jnp.maximum(u, 0.0) + jnp.log(1.0 + jnp.exp(-jnp.abs(u)))
    a = -jnp.exp(heads[0:1, :]) * dt
    cum = jnp.dot(
        jnp.where(past, 1.0, 0.0),
        a,
        preferred_element_type=jnp.float32,
        precision=lax.Precision.HIGHEST,
    )
    last = jnp.sum(a, axis=0, keepdims=True)
    mid = 0.5 * last
    dots = lax.dot_general(
        c_map, b_map, (((1,), (1,)), ((), ())), preferred_element_type=jnp.float32
    )
    dots = jnp.where(past, dots, 0.0).astype(jnp.bfloat16)
    b_flip = b_map.astype(jnp.float32).T.astype(jnp.bfloat16)
    shrink = split_sum(jnp.exp(mid - cum) * dt)
    rise = split_sum(jnp.exp(cum - mid))
    keep = (1 - table_start[0, 0]).astype(jnp.float32)
    half = jnp.exp(mid)
    vectors = split_sum(
        jnp.concatenate(
            [
                half,
                keep * half,
                keep * (half * half),
                heads[2:3, :],
                jnp.zeros((4, 128), jnp.float32),
            ],
            axis=0,
        )
    )
    pieces[0:tokens] = shrink
    pieces[tokens : 2 * tokens] = rise
    pieces[2 * tokens : 2 * tokens + 8] = vectors
    pieces[2 * tokens + 8 :] = jnp.zeros((8, 256), jnp.bfloat16)

    @pl.loop(0, chunks)
    def _(c):
        at = pl.multiple_of(c * chunk, chunk)
        pick = jnp.where(spacing[...] == c * (chunk // head_width), 1.0, 0.0)
        wide = jnp.dot(
            pieces[...], pick.astype(jnp.bfloat16), preferred_element_type=jnp.float32
        )
        ups = wide[tokens : 2 * tokens]
        x = x_got[:, :, pl.ds(at, chunk)].reshape(tokens, chunk).astype(jnp.float32)
        scaled = (x * wide[:tokens]).astype(jnp.bfloat16)
        leaving = wide[2 * tokens : 2 * tokens + 1] * jnp.dot(
            b_flip, scaled, preferred_element_type=jnp.float32
        )

        @pl.when(slab == 0)
        def _():
            leave[c] = leaving.astype(jnp.bfloat16)
            s_copy(c).start()

        y = jnp.dot(dots, scaled, preferred_element_type=jnp.float32) * ups
        y += wide[2 * tokens + 3 : 2 * tokens + 4] * x
        mixed[:, :, pl.ds(at, chunk)] = y.reshape(pack_size, block, chunk)

        @pl.when(slab > 0)
        def _():
            s_copy(c).wait_recv()
            got = enter[c]

            @pl.when(slab < ctx_size - 1)
            def _():
                decay = wide[2 * tokens + 2 : 2 * tokens + 3]
                leave[c] = (decay * got.astype(jnp.float32) + leaving).astype(jnp.bfloat16)
                s_copy(c).start()

            carried = jnp.dot(c_map, got, preferred_element_type=jnp.float32)
            carried *= ups * wide[2 * tokens + 1 : 2 * tokens + 2]
            mixed[:, :, pl.ds(at, chunk)] += carried.reshape(pack_size, block, chunk)

    for off in range(pack_size):
        peer = lax.rem(me + off, pack_size)
        if off > 0:
            z_copy(peer, peer).wait_recv()
        z = z_got[peer].astype(jnp.float32)
        g = mixed[peer] * (z / (1.0 + jnp.exp(-z)))
        scale = lax.rsqrt(jnp.mean(g * g, axis=-1, keepdims=True) + 1e-05)
        out[peer] = (g * scale * norm_gain[...]).astype(jnp.bfloat16)

    for off in range(1, pack_size):
        peer = lax.rem(me + off, pack_size)
        if not GATE_AFTER:
            x_copy(peer, me).wait_send()
        z_copy(peer, me).wait_send()

    @pl.when(slab < ctx_size - 1)
    def _():
        @pl.loop(0, chunks)
        def _(c):
            s_copy(c).wait_send()


def fused_body(
    signals, state_io, step_raw, row_target, table_start, log_rate, step_bias, skip_gain, norm_gain
):
    pack_size = lax.axis_size("pack")
    ctx_size = lax.axis_size("ctx")
    tokens = signals.shape[0]
    inner = signals.shape[1] // 2
    width = state_io.shape[1]
    state = width // 2
    head_count = log_rate.shape[0]
    block = tokens // pack_size
    chunks = inner // CHUNK
    vmem = pl.BlockSpec(memory_space=pltpu.VMEM)
    hbm = pl.BlockSpec(memory_space=pltpu.HBM)
    unsorted, order = pl.pallas_call(
        functools.partial(fused_kernel, pack_size, ctx_size, inner // head_count),
        out_shape=(
            jax.ShapeDtypeStruct((pack_size, block, inner), jnp.bfloat16),
            jax.ShapeDtypeStruct((tokens, tokens), jnp.bfloat16),
        ),
        in_specs=[hbm] * 9,
        out_specs=(vmem, vmem),
        scratch_shapes=[
            pltpu.VMEM((tokens, inner), jnp.bfloat16),
            pltpu.VMEM((tokens, inner), jnp.bfloat16),
            pltpu.VMEM((tokens, width), jnp.bfloat16),
            pltpu.VMEM((head_count, tokens), jnp.bfloat16),
            pltpu.SMEM((tokens // ROW,), jnp.int32),
            pltpu.SMEM((1, 1), jnp.int32),
            pltpu.VMEM((1, head_count), jnp.float32),
            pltpu.VMEM((1, head_count), jnp.float32),
            pltpu.VMEM((1, head_count), jnp.float32),
            pltpu.VMEM((1, inner), jnp.float32),
            pltpu.VMEM((2 * tokens + 16, 256), jnp.bfloat16),
            pltpu.VMEM((256, CHUNK), jnp.int32),
            pltpu.VMEM((tokens, width + 256), jnp.bfloat16),
            pltpu.VMEM((pack_size, block, inner + width + 256), jnp.bfloat16),
            pltpu.VMEM((pack_size, block, inner), jnp.bfloat16),
            pltpu.VMEM((pack_size, block, inner + width + 256), jnp.bfloat16),
            pltpu.VMEM((pack_size, block, inner), jnp.bfloat16),
            pltpu.VMEM((128, tokens), jnp.float32),
            pltpu.VMEM((pack_size, block, inner), jnp.float32),
            pltpu.VMEM((chunks, state, CHUNK), jnp.bfloat16),
            pltpu.VMEM((chunks, state, CHUNK), jnp.bfloat16),
            pltpu.SemaphoreType.DMA((10,)),
            pltpu.SemaphoreType.DMA((pack_size,)),
            pltpu.SemaphoreType.DMA((pack_size,)),
            pltpu.SemaphoreType.DMA((pack_size,)),
            pltpu.SemaphoreType.DMA((pack_size,)),
            pltpu.SemaphoreType.DMA((chunks,)),
            pltpu.SemaphoreType.DMA((chunks,)),
        ],
        compiler_params=pltpu.CompilerParams(
            collective_id=0, has_side_effects=True, vmem_limit_bytes=60 * 1024 * 1024
        ),
    )(
        signals,
        state_io,
        step_raw.T,
        row_target.reshape(-1),
        table_start,
        log_rate.reshape(1, -1),
        step_bias.reshape(1, -1),
        skip_gain.reshape(1, -1),
        norm_gain.reshape(1, -1),
    )
    return exact_permute(order, unsorted.reshape(tokens, inner))


def either_body(*arguments):
    one_group = arguments[0].shape[0] == GROUP and arguments[0].shape[1] % (2 * CHUNK) == 0
    return (fused_body if one_group else body)(*arguments)


def solution(mesh):
    return jax.shard_map(
        either_body,
        mesh=mesh,
        in_specs=(
            P(("pack", "ctx"), None),
            P(("pack", "ctx"), None),
            P(("pack", "ctx"), None),
            P("pack", "ctx", None),
            P("pack", "ctx"),
            P(),
            P(),
            P(),
            P(),
        ),
        out_specs=P(("pack", "ctx"), None),
        check_vma=False,
    )
```

```python
import functools

import jax
import jax.numpy as jnp
from jax import lax
from jax.experimental import pallas as pl
from jax.experimental.pallas import tpu as pltpu
from jax.sharding import PartitionSpec as P

GROUP = 128
ROW = 8
CHUNK = 512
GATE_AFTER = True
MESH = pl.DeviceIdType.MESH


def passed_along(block, axis, distance):
    devices = range(lax.axis_size(axis))
    route = [(i - distance, i) for i in devices if i - distance in devices]
    return lax.ppermute(block, axis, route)


def body(
    signals, state_io, step_raw, row_target, table_start, log_rate, step_bias, skip_gain, norm_gain
):
    pack_size = lax.axis_size("pack")
    ctx_size = lax.axis_size("ctx")
    row_count = row_target.shape[2]
    capacity = row_count // pack_size
    slot_count = pack_size * capacity
    inner_width = signals.shape[1] // 2
    head_count = log_rate.shape[0]
    head_width = inner_width // head_count
    state_width = state_io.shape[1] // 2
    token_count = row_count * ROW
    groups = token_count // GROUP
    targets = row_target.reshape(row_count)
    destination = targets // row_count
    row_index = jnp.arange(row_count, dtype=jnp.int32)
    earlier_rows = (destination[:, None] == destination[None, :]) & (
        row_index[None, :] < row_index[:, None]
    )
    earlier_count = jnp.sum(earlier_rows.astype(jnp.int32), axis=1)
    position = destination * capacity + earlier_count
    send_match = position[None, :] == jnp.arange(slot_count, dtype=jnp.int32)[:, None]
    filled = jnp.any(send_match, axis=1)
    source_row = jnp.where(
        filled, jnp.sum(jnp.where(send_match, row_index[None, :], 0), axis=1), row_count
    )
    send_slot = jnp.where(
        filled, jnp.sum(jnp.where(send_match, (targets % row_count)[None, :], 0), axis=1), -1
    )

    def outgoing(values):
        blocks = values.reshape(row_count, ROW, values.shape[1])
        return jnp.take(blocks, source_row, axis=0, mode="fill", fill_value=0)

    signal_got, io_got, raw_got, slot_got = (
        lax.all_to_all(
            outgoing(signals[:, inner_width:]), "pack", split_axis=0, concat_axis=0, tiled=True
        ),
        lax.all_to_all(outgoing(state_io), "pack", split_axis=0, concat_axis=0, tiled=True),
        lax.all_to_all(outgoing(step_raw), "pack", split_axis=0, concat_axis=0, tiled=True),
        lax.all_to_all(send_slot, "pack", split_axis=0, concat_axis=0, tiled=True),
    )
    slot_match = slot_got[None, :] == row_index[:, None]
    source_of = jnp.sum(
        jnp.where(slot_match, jnp.arange(slot_count, dtype=jnp.int32)[None, :], 0), axis=1
    )

    def arrange(values):
        return jnp.take(values, source_of, axis=0).reshape(token_count, values.shape[-1])

    signal_in = arrange(signal_got)
    io_rows = arrange(io_got)
    raw_rows = arrange(raw_got)
    inputs = signal_in.reshape(groups, GROUP, head_count, head_width)
    b_proj = io_rows[:, :state_width].reshape(groups, GROUP, state_width)
    c_proj = io_rows[:, state_width:].reshape(groups, GROUP, state_width)
    step_size = jax.nn.softplus(raw_rows.astype(jnp.float32) + step_bias).reshape(
        groups, GROUP, head_count
    )
    log_decay = -jnp.exp(log_rate) * step_size
    cumulative = jnp.cumsum(log_decay, axis=1)
    c_dot_b = jnp.einsum("kin,kjn->kij", c_proj, b_proj, preferred_element_type=jnp.float32)
    causal = jnp.arange(GROUP)[:, None] >= jnp.arange(GROUP)[None, :]
    per_head = cumulative.transpose(0, 2, 1)
    log_gaps = per_head[:, :, :, None] - per_head[:, :, None, :]
    decay_mask = jnp.exp(jnp.where(causal[None, None], log_gaps, -jnp.inf))
    scores = (c_dot_b[:, None] * decay_mask * step_size.transpose(0, 2, 1)[:, :, None, :]).astype(
        jnp.bfloat16
    )
    y_intra = jnp.einsum("khij,kjhp->kihp", scores, inputs, preferred_element_type=jnp.float32)
    to_end = jnp.exp(cumulative[:, -1:, :] - cumulative) * step_size
    weighted = (inputs.astype(jnp.float32) * to_end[..., None]).astype(jnp.bfloat16)
    local_state = jnp.einsum("kjhp,kjn->khpn", weighted, b_proj, preferred_element_type=jnp.float32)
    keep_flag = (1 - table_start.reshape(groups)).astype(jnp.float32)
    group_decay = jnp.exp(cumulative[:, -1, :])
    carry_gain = []
    carry_base = []
    gain_now = keep_flag[0] * jnp.ones((head_count,), jnp.float32)
    base_now = jnp.zeros((head_count, head_width, state_width), jnp.float32)
    for group_id in range(groups):
        if group_id > 0:
            gain_now = keep_flag[group_id] * (group_decay[group_id - 1] * gain_now)
            base_now = keep_flag[group_id] * (
                group_decay[group_id - 1][:, None, None] * base_now + local_state[group_id - 1]
            )
        carry_gain.append(gain_now)
        carry_base.append(base_now)
    leave_gain = group_decay[-1] * gain_now
    leave_base = group_decay[-1][:, None, None] * base_now + local_state[-1]
    incoming = jnp.zeros((head_count, head_width, state_width), jnp.float32)
    for hop_index in range(ctx_size - 1):
        incoming = passed_along(leave_gain[:, None, None] * incoming + leave_base, "ctx", 1)
    entering = jnp.stack(carry_gain)[:, :, None, None] * incoming[None] + jnp.stack(carry_base)
    y_state = jnp.exp(cumulative)[..., None] * jnp.einsum(
        "kin,khpn->kihp", c_proj.astype(jnp.float32), entering, precision=lax.Precision.HIGHEST
    )
    mixed = y_intra + y_state + skip_gain[None, None, :, None] * inputs.astype(jnp.float32)
    mixed = mixed.reshape(token_count, inner_width)
    gate_got = lax.all_to_all(
        outgoing(signals[:, :inner_width]), "pack", split_axis=0, concat_axis=0, tiled=True
    )
    gate_in = arrange(gate_got)
    gated = mixed * jax.nn.silu(gate_in.astype(jnp.float32))
    result = gated * lax.rsqrt(jnp.mean(gated * gated, axis=-1, keepdims=True) + 1e-05) * norm_gain
    return result.astype(jnp.bfloat16)


def exact_permute(onehot, values):
    return jnp.dot(onehot, values, preferred_element_type=jnp.float32).astype(jnp.bfloat16)


def split_sum(values):
    high = values.astype(jnp.bfloat16)
    low = (values - high.astype(jnp.float32)).astype(jnp.bfloat16)
    return jnp.concatenate([high, low], axis=1)


def fused_kernel(
    pack_size,
    ctx_size,
    head_width,
    signals_hbm,
    state_io_hbm,
    step_flip_hbm,
    row_target_hbm,
    table_start_hbm,
    log_rate_hbm,
    step_bias_hbm,
    skip_gain_hbm,
    norm_gain_hbm,
    out,
    order,
    x_in,
    z_in,
    state_io,
    step_flip,
    row_target,
    table_start,
    log_rate,
    step_bias,
    skip_gain,
    norm_gain,
    pieces,
    spacing,
    small,
    x_stage,
    z_stage,
    x_got,
    z_got,
    heads,
    mixed,
    leave,
    enter,
    load,
    x_send,
    x_recv,
    z_send,
    z_recv,
    s_send,
    s_recv,
):
    tokens = GROUP
    rows = tokens // ROW
    inner = norm_gain.shape[1]
    head_count = log_rate.shape[1]
    width = state_io.shape[1]
    state = width // 2
    block = tokens // pack_size
    chunk = CHUNK
    chunks = inner // chunk
    me = lax.axis_index("pack")
    slab = lax.axis_index("ctx")
    loads = [
        pltpu.make_async_copy(source, held, load.at[i])
        for i, (source, held) in enumerate(
            (
                (row_target_hbm, row_target),
                (signals_hbm.at[:, pl.ds(inner, inner)], x_in),
                (state_io_hbm, state_io),
                (step_flip_hbm, step_flip),
                (signals_hbm.at[:, pl.ds(0, inner)], z_in),
                (table_start_hbm, table_start),
                (log_rate_hbm, log_rate),
                (step_bias_hbm, step_bias),
                (skip_gain_hbm, skip_gain),
                (norm_gain_hbm, norm_gain),
            )
        )
    ]
    for copy in loads:
        copy.start()
    barrier = pltpu.get_barrier_semaphore()
    for off in range(1, pack_size):
        pl.semaphore_signal(
            barrier, inc=1, device_id={"pack": lax.rem(me + off, pack_size)}, device_id_type=MESH
        )
    for off in range(1, ctx_size):
        pl.semaphore_signal(
            barrier, inc=1, device_id={"ctx": lax.rem(slab + off, ctx_size)}, device_id_type=MESH
        )

    lane = lax.broadcasted_iota(jnp.int32, (tokens, tokens), 1)
    sub = lax.broadcasted_iota(jnp.int32, (tokens, tokens), 0)
    head = lax.broadcasted_iota(jnp.int32, (256, chunk), 0) % 128
    column = lax.broadcasted_iota(jnp.int32, (256, chunk), 1) // head_width
    spacing[...] = head - column
    loads[0].wait()
    goal_lane = jnp.zeros((1, tokens), jnp.int32)
    goal_rows = []
    slot_rows = []
    for j in range(rows):
        target = row_target[j]
        goal = target // rows
        goal_lane = jnp.where(lane[:1] // ROW == j, goal, goal_lane)
        goal_rows.append(jnp.full((ROW, tokens), goal, jnp.int32))
        slot_rows.append(jnp.full((ROW, tokens), target - goal * rows, jnp.int32))
    goal_sub = jnp.concatenate(goal_rows, axis=0)
    slot_sub = jnp.concatenate(slot_rows, axis=0)
    earlier = (goal_sub == goal_lane) & (sub // ROW < lane // ROW) & (sub % ROW == 0)
    earlier = jnp.sum(jnp.where(earlier, 1.0, 0.0), axis=0, keepdims=True).astype(jnp.int32)
    place = (goal_lane * (rows // pack_size) + earlier) * ROW + lane[:1] % ROW
    send_order = jnp.where(sub == place, 1.0, 0.0).astype(jnp.bfloat16)
    for copy in loads[1:4]:
        copy.wait()
    small[:, :width] = state_io[...]
    heads[...] = jnp.zeros(heads.shape, jnp.float32)
    heads[:head_count] = step_flip[...].astype(jnp.float32)
    small[:, width : width + 128] = heads[...].T.astype(jnp.bfloat16)
    small[:, width + 128 :] = (slot_sub * ROW + sub % ROW).astype(jnp.float32).astype(jnp.bfloat16)
    half_chunks = chunks // 2
    cut = half_chunks * chunk

    def stage_x(c):
        at = pl.multiple_of(c * chunk, chunk)
        x_stage[:, :, pl.ds(at, chunk)] = exact_permute(
            send_order, x_in[:, pl.ds(at, chunk)]
        ).reshape(pack_size, block, chunk)

    pl.loop(0, half_chunks)(stage_x)
    pl.semaphore_wait(barrier, pack_size + ctx_size - 2)

    def x_copy(peer, slot, part):
        columns = pl.ds(0, cut) if part == 0 else pl.ds(cut, x_stage.shape[2] - cut)
        return pltpu.make_async_remote_copy(
            src_ref=x_stage.at[peer, :, columns],
            dst_ref=x_got.at[slot, :, columns],
            send_sem=x_send.at[part, peer],
            recv_sem=x_recv.at[part, slot],
            device_id={"pack": peer},
            device_id_type=MESH,
        )

    def z_copy(peer, slot):
        return pltpu.make_async_remote_copy(
            src_ref=z_stage.at[peer],
            dst_ref=z_got.at[slot],
            send_sem=z_send.at[peer],
            recv_sem=z_recv.at[slot],
            device_id={"pack": peer},
            device_id_type=MESH,
        )

    def s_copy(c):
        return pltpu.make_async_remote_copy(
            src_ref=leave.at[c],
            dst_ref=enter.at[c],
            send_sem=s_send.at[c],
            recv_sem=s_recv.at[c],
            device_id={"ctx": lax.rem(slab + 1, ctx_size)},
            device_id_type=MESH,
        )

    for off in range(1, pack_size):
        x_copy(lax.rem(me + off, pack_size), me, 0).start()
    x_stage[:, :, inner:] = exact_permute(send_order, small[...]).reshape(
        pack_size, block, width + 256
    )

    pl.loop(half_chunks, chunks)(stage_x)
    for off in range(1, pack_size):
        x_copy(lax.rem(me + off, pack_size), me, 1).start()

    for copy in loads[4:]:
        copy.wait()

    @pl.loop(0, chunks)
    def _(c):
        at = pl.multiple_of(c * chunk, chunk)
        z_stage[:, :, pl.ds(at, chunk)] = exact_permute(
            send_order, z_in[:, pl.ds(at, chunk)]
        ).reshape(pack_size, block, chunk)

    x_got[me] = x_stage[me]
    z_got[me] = z_stage[me]
    if GATE_AFTER:
        for off in range(1, pack_size):
            for part in range(2):
                x_copy(lax.rem(me + off, pack_size), me, part).wait_send()
    for off in range(1, pack_size):
        z_copy(lax.rem(me + off, pack_size), me).start()
    for off in range(1, pack_size):
        peer = lax.rem(me + off, pack_size)
        for part in range(2):
            x_copy(peer, peer, part).wait_recv()

    heads[0:8] = jnp.zeros((8, 128), jnp.float32)
    heads[0:1, :head_count] = log_rate[...]
    heads[1:2, :head_count] = step_bias[...]
    heads[2:3, :head_count] = skip_gain[...]
    maps = x_got[:, :, inner : inner + width].reshape(tokens, width)
    b_map = maps[:, :state]
    c_map = maps[:, state:]
    raw = x_got[:, :, inner + width : inner + width + 128].reshape(tokens, 128)
    spot = x_got[:, :, inner + width + 128 :].reshape(tokens, 128).astype(jnp.float32)
    spot_lane = spot.T
    past = spot_lane <= spot
    order[...] = jnp.where(spot_lane == sub.astype(jnp.float32), 1.0, 0.0).astype(jnp.bfloat16)
    u = raw.astype(jnp.float32) + heads[1:2, :]
    dt = jnp.maximum(u, 0.0) + jnp.log(1.0 + jnp.exp(-jnp.abs(u)))
    a = -jnp.exp(heads[0:1, :]) * dt
    cum = jnp.dot(
        jnp.where(past, 1.0, 0.0),
        a,
        preferred_element_type=jnp.float32,
        precision=lax.Precision.HIGHEST,
    )
    last = jnp.sum(a, axis=0, keepdims=True)
    mid = 0.5 * last
    dots = lax.dot_general(
        c_map, b_map, (((1,), (1,)), ((), ())), preferred_element_type=jnp.float32
    )
    dots = jnp.where(past, dots, 0.0).astype(jnp.bfloat16)
    b_flip = b_map.astype(jnp.float32).T.astype(jnp.bfloat16)
    shrink = split_sum(jnp.exp(mid - cum) * dt)
    rise = split_sum(jnp.exp(cum - mid))
    keep = (1 - table_start[0, 0]).astype(jnp.float32)
    half = jnp.exp(mid)
    vectors = split_sum(
        jnp.concatenate(
            [
                half,
                keep * half,
                keep * (half * half),
                heads[2:3, :],
                jnp.zeros((4, 128), jnp.float32),
            ],
            axis=0,
        )
    )
    pieces[0:tokens] = shrink
    pieces[tokens : 2 * tokens] = rise
    pieces[2 * tokens : 2 * tokens + 8] = vectors
    pieces[2 * tokens + 8 :] = jnp.zeros((8, 256), jnp.bfloat16)

    @pl.loop(0, chunks)
    def _(c):
        at = pl.multiple_of(c * chunk, chunk)
        pick = jnp.where(spacing[...] == c * (chunk // head_width), 1.0, 0.0)
        wide = jnp.dot(
            pieces[...], pick.astype(jnp.bfloat16), preferred_element_type=jnp.float32
        )
        ups = wide[tokens : 2 * tokens]
        x = x_got[:, :, pl.ds(at, chunk)].reshape(tokens, chunk).astype(jnp.float32)
        scaled = (x * wide[:tokens]).astype(jnp.bfloat16)
        leaving = wide[2 * tokens : 2 * tokens + 1] * jnp.dot(
            b_flip, scaled, preferred_element_type=jnp.float32
        )

        @pl.when(slab == 0)
        def _():
            leave[c] = leaving.astype(jnp.bfloat16)
            s_copy(c).start()

        y = jnp.dot(dots, scaled, preferred_element_type=jnp.float32) * ups
        y += wide[2 * tokens + 3 : 2 * tokens + 4] * x
        mixed[:, :, pl.ds(at, chunk)] = y.reshape(pack_size, block, chunk)

        @pl.when(slab > 0)
        def _():
            s_copy(c).wait_recv()
            got = enter[c]

            @pl.when(slab < ctx_size - 1)
            def _():
                decay = wide[2 * tokens + 2 : 2 * tokens + 3]
                leave[c] = (decay * got.astype(jnp.float32) + leaving).astype(jnp.bfloat16)
                s_copy(c).start()

            carried = jnp.dot(c_map, got, preferred_element_type=jnp.float32)
            carried *= ups * wide[2 * tokens + 1 : 2 * tokens + 2]
            mixed[:, :, pl.ds(at, chunk)] += carried.reshape(pack_size, block, chunk)

    for off in range(pack_size):
        peer = lax.rem(me + off, pack_size)
        if off > 0:
            z_copy(peer, peer).wait_recv()
        z = z_got[peer].astype(jnp.float32)
        g = mixed[peer] * (z / (1.0 + jnp.exp(-z)))
        scale = lax.rsqrt(jnp.mean(g * g, axis=-1, keepdims=True) + 1e-05)
        out[peer] = (g * scale * norm_gain[...]).astype(jnp.bfloat16)

    for off in range(1, pack_size):
        peer = lax.rem(me + off, pack_size)
        if not GATE_AFTER:
            for part in range(2):
                x_copy(peer, me, part).wait_send()
        z_copy(peer, me).wait_send()

    @pl.when(slab < ctx_size - 1)
    def _():
        @pl.loop(0, chunks)
        def _(c):
            s_copy(c).wait_send()


def fused_body(
    signals, state_io, step_raw, row_target, table_start, log_rate, step_bias, skip_gain, norm_gain
):
    pack_size = lax.axis_size("pack")
    ctx_size = lax.axis_size("ctx")
    tokens = signals.shape[0]
    inner = signals.shape[1] // 2
    width = state_io.shape[1]
    state = width // 2
    head_count = log_rate.shape[0]
    block = tokens // pack_size
    chunks = inner // CHUNK
    vmem = pl.BlockSpec(memory_space=pltpu.VMEM)
    hbm = pl.BlockSpec(memory_space=pltpu.HBM)
    unsorted, order = pl.pallas_call(
        functools.partial(fused_kernel, pack_size, ctx_size, inner // head_count),
        out_shape=(
            jax.ShapeDtypeStruct((pack_size, block, inner), jnp.bfloat16),
            jax.ShapeDtypeStruct((tokens, tokens), jnp.bfloat16),
        ),
        in_specs=[hbm] * 9,
        out_specs=(vmem, vmem),
        scratch_shapes=[
            pltpu.VMEM((tokens, inner), jnp.bfloat16),
            pltpu.VMEM((tokens, inner), jnp.bfloat16),
            pltpu.VMEM((tokens, width), jnp.bfloat16),
            pltpu.VMEM((head_count, tokens), jnp.bfloat16),
            pltpu.SMEM((tokens // ROW,), jnp.int32),
            pltpu.SMEM((1, 1), jnp.int32),
            pltpu.VMEM((1, head_count), jnp.float32),
            pltpu.VMEM((1, head_count), jnp.float32),
            pltpu.VMEM((1, head_count), jnp.float32),
            pltpu.VMEM((1, inner), jnp.float32),
            pltpu.VMEM((2 * tokens + 16, 256), jnp.bfloat16),
            pltpu.VMEM((256, CHUNK), jnp.int32),
            pltpu.VMEM((tokens, width + 256), jnp.bfloat16),
            pltpu.VMEM((pack_size, block, inner + width + 256), jnp.bfloat16),
            pltpu.VMEM((pack_size, block, inner), jnp.bfloat16),
            pltpu.VMEM((pack_size, block, inner + width + 256), jnp.bfloat16),
            pltpu.VMEM((pack_size, block, inner), jnp.bfloat16),
            pltpu.VMEM((128, tokens), jnp.float32),
            pltpu.VMEM((pack_size, block, inner), jnp.float32),
            pltpu.VMEM((chunks, state, CHUNK), jnp.bfloat16),
            pltpu.VMEM((chunks, state, CHUNK), jnp.bfloat16),
            pltpu.SemaphoreType.DMA((10,)),
            pltpu.SemaphoreType.DMA((2, pack_size)),
            pltpu.SemaphoreType.DMA((2, pack_size)),
            pltpu.SemaphoreType.DMA((pack_size,)),
            pltpu.SemaphoreType.DMA((pack_size,)),
            pltpu.SemaphoreType.DMA((chunks,)),
            pltpu.SemaphoreType.DMA((chunks,)),
        ],
        compiler_params=pltpu.CompilerParams(
            collective_id=0, has_side_effects=True, vmem_limit_bytes=60 * 1024 * 1024
        ),
    )(
        signals,
        state_io,
        step_raw.T,
        row_target.reshape(-1),
        table_start,
        log_rate.reshape(1, -1),
        step_bias.reshape(1, -1),
        skip_gain.reshape(1, -1),
        norm_gain.reshape(1, -1),
    )
    return exact_permute(order, unsorted.reshape(tokens, inner))


def either_body(*arguments):
    one_group = arguments[0].shape[0] == GROUP and arguments[0].shape[1] % (2 * CHUNK) == 0
    return (fused_body if one_group else body)(*arguments)


def solution(mesh):
    return jax.shard_map(
        either_body,
        mesh=mesh,
        in_specs=(
            P(("pack", "ctx"), None),
            P(("pack", "ctx"), None),
            P(("pack", "ctx"), None),
            P("pack", "ctx", None),
            P("pack", "ctx"),
            P(),
            P(),
            P(),
            P(),
        ),
        out_specs=P(("pack", "ctx"), None),
        check_vma=False,
    )
```

```python
import functools

import jax
import jax.numpy as jnp
from jax import lax
from jax.experimental import pallas as pl
from jax.experimental.pallas import tpu as pltpu
from jax.sharding import PartitionSpec as P

GROUP = 128
ROW = 8
CHUNK = 512
GATE_AFTER = True
MESH = pl.DeviceIdType.MESH


def passed_along(block, axis, distance):
    devices = range(lax.axis_size(axis))
    route = [(i - distance, i) for i in devices if i - distance in devices]
    return lax.ppermute(block, axis, route)


def body(
    signals, state_io, step_raw, row_target, table_start, log_rate, step_bias, skip_gain, norm_gain
):
    pack_size = lax.axis_size("pack")
    ctx_size = lax.axis_size("ctx")
    row_count = row_target.shape[2]
    capacity = row_count // pack_size
    slot_count = pack_size * capacity
    inner_width = signals.shape[1] // 2
    head_count = log_rate.shape[0]
    head_width = inner_width // head_count
    state_width = state_io.shape[1] // 2
    token_count = row_count * ROW
    groups = token_count // GROUP
    targets = row_target.reshape(row_count)
    destination = targets // row_count
    row_index = jnp.arange(row_count, dtype=jnp.int32)
    earlier_rows = (destination[:, None] == destination[None, :]) & (
        row_index[None, :] < row_index[:, None]
    )
    earlier_count = jnp.sum(earlier_rows.astype(jnp.int32), axis=1)
    position = destination * capacity + earlier_count
    send_match = position[None, :] == jnp.arange(slot_count, dtype=jnp.int32)[:, None]
    filled = jnp.any(send_match, axis=1)
    source_row = jnp.where(
        filled, jnp.sum(jnp.where(send_match, row_index[None, :], 0), axis=1), row_count
    )
    send_slot = jnp.where(
        filled, jnp.sum(jnp.where(send_match, (targets % row_count)[None, :], 0), axis=1), -1
    )

    def outgoing(values):
        blocks = values.reshape(row_count, ROW, values.shape[1])
        return jnp.take(blocks, source_row, axis=0, mode="fill", fill_value=0)

    signal_got, io_got, raw_got, slot_got = (
        lax.all_to_all(
            outgoing(signals[:, inner_width:]), "pack", split_axis=0, concat_axis=0, tiled=True
        ),
        lax.all_to_all(outgoing(state_io), "pack", split_axis=0, concat_axis=0, tiled=True),
        lax.all_to_all(outgoing(step_raw), "pack", split_axis=0, concat_axis=0, tiled=True),
        lax.all_to_all(send_slot, "pack", split_axis=0, concat_axis=0, tiled=True),
    )
    slot_match = slot_got[None, :] == row_index[:, None]
    source_of = jnp.sum(
        jnp.where(slot_match, jnp.arange(slot_count, dtype=jnp.int32)[None, :], 0), axis=1
    )

    def arrange(values):
        return jnp.take(values, source_of, axis=0).reshape(token_count, values.shape[-1])

    signal_in = arrange(signal_got)
    io_rows = arrange(io_got)
    raw_rows = arrange(raw_got)
    inputs = signal_in.reshape(groups, GROUP, head_count, head_width)
    b_proj = io_rows[:, :state_width].reshape(groups, GROUP, state_width)
    c_proj = io_rows[:, state_width:].reshape(groups, GROUP, state_width)
    step_size = jax.nn.softplus(raw_rows.astype(jnp.float32) + step_bias).reshape(
        groups, GROUP, head_count
    )
    log_decay = -jnp.exp(log_rate) * step_size
    cumulative = jnp.cumsum(log_decay, axis=1)
    c_dot_b = jnp.einsum("kin,kjn->kij", c_proj, b_proj, preferred_element_type=jnp.float32)
    causal = jnp.arange(GROUP)[:, None] >= jnp.arange(GROUP)[None, :]
    per_head = cumulative.transpose(0, 2, 1)
    log_gaps = per_head[:, :, :, None] - per_head[:, :, None, :]
    decay_mask = jnp.exp(jnp.where(causal[None, None], log_gaps, -jnp.inf))
    scores = (c_dot_b[:, None] * decay_mask * step_size.transpose(0, 2, 1)[:, :, None, :]).astype(
        jnp.bfloat16
    )
    y_intra = jnp.einsum("khij,kjhp->kihp", scores, inputs, preferred_element_type=jnp.float32)
    to_end = jnp.exp(cumulative[:, -1:, :] - cumulative) * step_size
    weighted = (inputs.astype(jnp.float32) * to_end[..., None]).astype(jnp.bfloat16)
    local_state = jnp.einsum("kjhp,kjn->khpn", weighted, b_proj, preferred_element_type=jnp.float32)
    keep_flag = (1 - table_start.reshape(groups)).astype(jnp.float32)
    group_decay = jnp.exp(cumulative[:, -1, :])
    carry_gain = []
    carry_base = []
    gain_now = keep_flag[0] * jnp.ones((head_count,), jnp.float32)
    base_now = jnp.zeros((head_count, head_width, state_width), jnp.float32)
    for group_id in range(groups):
        if group_id > 0:
            gain_now = keep_flag[group_id] * (group_decay[group_id - 1] * gain_now)
            base_now = keep_flag[group_id] * (
                group_decay[group_id - 1][:, None, None] * base_now + local_state[group_id - 1]
            )
        carry_gain.append(gain_now)
        carry_base.append(base_now)
    leave_gain = group_decay[-1] * gain_now
    leave_base = group_decay[-1][:, None, None] * base_now + local_state[-1]
    incoming = jnp.zeros((head_count, head_width, state_width), jnp.float32)
    for hop_index in range(ctx_size - 1):
        incoming = passed_along(leave_gain[:, None, None] * incoming + leave_base, "ctx", 1)
    entering = jnp.stack(carry_gain)[:, :, None, None] * incoming[None] + jnp.stack(carry_base)
    y_state = jnp.exp(cumulative)[..., None] * jnp.einsum(
        "kin,khpn->kihp", c_proj.astype(jnp.float32), entering, precision=lax.Precision.HIGHEST
    )
    mixed = y_intra + y_state + skip_gain[None, None, :, None] * inputs.astype(jnp.float32)
    mixed = mixed.reshape(token_count, inner_width)
    gate_got = lax.all_to_all(
        outgoing(signals[:, :inner_width]), "pack", split_axis=0, concat_axis=0, tiled=True
    )
    gate_in = arrange(gate_got)
    gated = mixed * jax.nn.silu(gate_in.astype(jnp.float32))
    result = gated * lax.rsqrt(jnp.mean(gated * gated, axis=-1, keepdims=True) + 1e-05) * norm_gain
    return result.astype(jnp.bfloat16)


def exact_permute(onehot, values):
    return jnp.dot(onehot, values, preferred_element_type=jnp.float32).astype(jnp.bfloat16)


def split_sum(values):
    high = values.astype(jnp.bfloat16)
    low = (values - high.astype(jnp.float32)).astype(jnp.bfloat16)
    return jnp.concatenate([high, low], axis=1)


def fused_kernel(
    pack_size,
    ctx_size,
    head_width,
    signals_hbm,
    state_io_hbm,
    step_flip_hbm,
    row_target_hbm,
    table_start_hbm,
    log_rate_hbm,
    step_bias_hbm,
    skip_gain_hbm,
    norm_gain_hbm,
    out,
    order,
    x_in,
    z_in,
    state_io,
    step_flip,
    row_target,
    table_start,
    log_rate,
    step_bias,
    skip_gain,
    norm_gain,
    pieces,
    spacing,
    small,
    x_stage,
    z_stage,
    x_got,
    z_got,
    heads,
    mixed,
    leave,
    enter,
    finished,
    load,
    store,
    x_send,
    x_recv,
    z_send,
    z_recv,
    s_send,
    s_recv,
):
    tokens = GROUP
    rows = tokens // ROW
    inner = norm_gain.shape[1]
    head_count = log_rate.shape[1]
    width = state_io.shape[1]
    state = width // 2
    block = tokens // pack_size
    chunk = CHUNK
    chunks = inner // chunk
    me = lax.axis_index("pack")
    slab = lax.axis_index("ctx")
    loads = [
        pltpu.make_async_copy(source, held, load.at[i])
        for i, (source, held) in enumerate(
            (
                (row_target_hbm, row_target),
                (signals_hbm.at[:, pl.ds(inner, inner)], x_in),
                (state_io_hbm, state_io),
                (step_flip_hbm, step_flip),
                (signals_hbm.at[:, pl.ds(0, inner)], z_in),
                (table_start_hbm, table_start),
                (log_rate_hbm, log_rate),
                (step_bias_hbm, step_bias),
                (skip_gain_hbm, skip_gain),
                (norm_gain_hbm, norm_gain),
            )
        )
    ]
    for copy in loads:
        copy.start()
    barrier = pltpu.get_barrier_semaphore()
    for off in range(1, pack_size):
        pl.semaphore_signal(
            barrier, inc=1, device_id={"pack": lax.rem(me + off, pack_size)}, device_id_type=MESH
        )
    for off in range(1, ctx_size):
        pl.semaphore_signal(
            barrier, inc=1, device_id={"ctx": lax.rem(slab + off, ctx_size)}, device_id_type=MESH
        )

    lane = lax.broadcasted_iota(jnp.int32, (tokens, tokens), 1)
    sub = lax.broadcasted_iota(jnp.int32, (tokens, tokens), 0)
    head = lax.broadcasted_iota(jnp.int32, (256, chunk), 0) % 128
    column = lax.broadcasted_iota(jnp.int32, (256, chunk), 1) // head_width
    spacing[...] = head - column
    loads[0].wait()
    goal_lane = jnp.zeros((1, tokens), jnp.int32)
    goal_rows = []
    slot_rows = []
    for j in range(rows):
        target = row_target[j]
        goal = target // rows
        goal_lane = jnp.where(lane[:1] // ROW == j, goal, goal_lane)
        goal_rows.append(jnp.full((ROW, tokens), goal, jnp.int32))
        slot_rows.append(jnp.full((ROW, tokens), target - goal * rows, jnp.int32))
    goal_sub = jnp.concatenate(goal_rows, axis=0)
    slot_sub = jnp.concatenate(slot_rows, axis=0)
    earlier = (goal_sub == goal_lane) & (sub // ROW < lane // ROW) & (sub % ROW == 0)
    earlier = jnp.sum(jnp.where(earlier, 1.0, 0.0), axis=0, keepdims=True).astype(jnp.int32)
    place = (goal_lane * (rows // pack_size) + earlier) * ROW + lane[:1] % ROW
    send_order = jnp.where(sub == place, 1.0, 0.0).astype(jnp.bfloat16)
    for copy in loads[1:4]:
        copy.wait()
    small[:, :width] = state_io[...]
    heads[...] = jnp.zeros(heads.shape, jnp.float32)
    heads[:head_count] = step_flip[...].astype(jnp.float32)
    small[:, width : width + 128] = heads[...].T.astype(jnp.bfloat16)
    small[:, width + 128 :] = (slot_sub * ROW + sub % ROW).astype(jnp.float32).astype(jnp.bfloat16)
    half_chunks = chunks // 2
    cut = half_chunks * chunk

    def stage_x(c):
        at = pl.multiple_of(c * chunk, chunk)
        x_stage[:, :, pl.ds(at, chunk)] = exact_permute(
            send_order, x_in[:, pl.ds(at, chunk)]
        ).reshape(pack_size, block, chunk)

    pl.loop(0, half_chunks)(stage_x)
    pl.semaphore_wait(barrier, pack_size + ctx_size - 2)

    def x_copy(peer, slot, part):
        columns = pl.ds(0, cut) if part == 0 else pl.ds(cut, x_stage.shape[2] - cut)
        return pltpu.make_async_remote_copy(
            src_ref=x_stage.at[peer, :, columns],
            dst_ref=x_got.at[slot, :, columns],
            send_sem=x_send.at[part, peer],
            recv_sem=x_recv.at[part, slot],
            device_id={"pack": peer},
            device_id_type=MESH,
        )

    def z_copy(peer, slot):
        return pltpu.make_async_remote_copy(
            src_ref=z_stage.at[peer],
            dst_ref=z_got.at[slot],
            send_sem=z_send.at[peer],
            recv_sem=z_recv.at[slot],
            device_id={"pack": peer},
            device_id_type=MESH,
        )

    def s_copy(c):
        return pltpu.make_async_remote_copy(
            src_ref=leave.at[c],
            dst_ref=enter.at[c],
            send_sem=s_send.at[c],
            recv_sem=s_recv.at[c],
            device_id={"ctx": lax.rem(slab + 1, ctx_size)},
            device_id_type=MESH,
        )

    for off in range(1, pack_size):
        x_copy(lax.rem(me + off, pack_size), me, 0).start()
    x_stage[:, :, inner:] = exact_permute(send_order, small[...]).reshape(
        pack_size, block, width + 256
    )

    pl.loop(half_chunks, chunks)(stage_x)
    for off in range(1, pack_size):
        x_copy(lax.rem(me + off, pack_size), me, 1).start()

    for copy in loads[4:]:
        copy.wait()

    @pl.loop(0, chunks)
    def _(c):
        at = pl.multiple_of(c * chunk, chunk)
        z_stage[:, :, pl.ds(at, chunk)] = exact_permute(
            send_order, z_in[:, pl.ds(at, chunk)]
        ).reshape(pack_size, block, chunk)

    x_got[me] = x_stage[me]
    z_got[me] = z_stage[me]
    if GATE_AFTER:
        for off in range(1, pack_size):
            for part in range(2):
                x_copy(lax.rem(me + off, pack_size), me, part).wait_send()
    for off in range(1, pack_size):
        z_copy(lax.rem(me + off, pack_size), me).start()
    for off in range(1, pack_size):
        peer = lax.rem(me + off, pack_size)
        for part in range(2):
            x_copy(peer, peer, part).wait_recv()

    heads[0:8] = jnp.zeros((8, 128), jnp.float32)
    heads[0:1, :head_count] = log_rate[...]
    heads[1:2, :head_count] = step_bias[...]
    heads[2:3, :head_count] = skip_gain[...]
    maps = x_got[:, :, inner : inner + width].reshape(tokens, width)
    b_map = maps[:, :state]
    c_map = maps[:, state:]
    raw = x_got[:, :, inner + width : inner + width + 128].reshape(tokens, 128)
    spot = x_got[:, :, inner + width + 128 :].reshape(tokens, 128).astype(jnp.float32)
    spot_lane = spot.T
    past = spot_lane <= spot
    order[...] = jnp.where(spot_lane == sub.astype(jnp.float32), 1.0, 0.0).astype(jnp.bfloat16)
    u = raw.astype(jnp.float32) + heads[1:2, :]
    dt = jnp.maximum(u, 0.0) + jnp.log(1.0 + jnp.exp(-jnp.abs(u)))
    a = -jnp.exp(heads[0:1, :]) * dt
    cum = jnp.dot(
        jnp.where(past, 1.0, 0.0),
        a,
        preferred_element_type=jnp.float32,
        precision=lax.Precision.HIGHEST,
    )
    last = jnp.sum(a, axis=0, keepdims=True)
    mid = 0.5 * last
    dots = lax.dot_general(
        c_map, b_map, (((1,), (1,)), ((), ())), preferred_element_type=jnp.float32
    )
    dots = jnp.where(past, dots, 0.0).astype(jnp.bfloat16)
    b_flip = b_map.astype(jnp.float32).T.astype(jnp.bfloat16)
    shrink = split_sum(jnp.exp(mid - cum) * dt)
    rise = split_sum(jnp.exp(cum - mid))
    keep = (1 - table_start[0, 0]).astype(jnp.float32)
    half = jnp.exp(mid)
    vectors = split_sum(
        jnp.concatenate(
            [
                half,
                keep * half,
                keep * (half * half),
                heads[2:3, :],
                jnp.zeros((4, 128), jnp.float32),
            ],
            axis=0,
        )
    )
    pieces[0:tokens] = shrink
    pieces[tokens : 2 * tokens] = rise
    pieces[2 * tokens : 2 * tokens + 8] = vectors
    pieces[2 * tokens + 8 :] = jnp.zeros((8, 256), jnp.bfloat16)

    @pl.loop(0, chunks)
    def _(c):
        at = pl.multiple_of(c * chunk, chunk)
        pick = jnp.where(spacing[...] == c * (chunk // head_width), 1.0, 0.0)
        wide = jnp.dot(
            pieces[...], pick.astype(jnp.bfloat16), preferred_element_type=jnp.float32
        )
        ups = wide[tokens : 2 * tokens]
        x = x_got[:, :, pl.ds(at, chunk)].reshape(tokens, chunk).astype(jnp.float32)
        scaled = (x * wide[:tokens]).astype(jnp.bfloat16)
        leaving = wide[2 * tokens : 2 * tokens + 1] * jnp.dot(
            b_flip, scaled, preferred_element_type=jnp.float32
        )

        @pl.when(slab == 0)
        def _():
            leave[c] = leaving.astype(jnp.bfloat16)
            s_copy(c).start()

        y = jnp.dot(dots, scaled, preferred_element_type=jnp.float32) * ups
        y += wide[2 * tokens + 3 : 2 * tokens + 4] * x
        mixed[:, :, pl.ds(at, chunk)] = y.reshape(pack_size, block, chunk)

        @pl.when(slab > 0)
        def _():
            s_copy(c).wait_recv()
            got = enter[c]

            @pl.when(slab < ctx_size - 1)
            def _():
                decay = wide[2 * tokens + 2 : 2 * tokens + 3]
                leave[c] = (decay * got.astype(jnp.float32) + leaving).astype(jnp.bfloat16)
                s_copy(c).start()

            carried = jnp.dot(c_map, got, preferred_element_type=jnp.float32)
            carried *= ups * wide[2 * tokens + 1 : 2 * tokens + 2]
            mixed[:, :, pl.ds(at, chunk)] += carried.reshape(pack_size, block, chunk)

    for off in range(pack_size):
        peer = lax.rem(me + off, pack_size)
        if off > 0:
            z_copy(peer, peer).wait_recv()
        z = z_got[peer].astype(jnp.float32)
        g = mixed[peer] * (z / (1.0 + jnp.exp(-z)))
        scale = lax.rsqrt(jnp.mean(g * g, axis=-1, keepdims=True) + 1e-05)
        finished[peer] = (g * scale * norm_gain[...]).astype(jnp.bfloat16)
        pltpu.make_async_copy(finished.at[peer], out.at[peer], store.at[peer]).start()

    for off in range(1, pack_size):
        peer = lax.rem(me + off, pack_size)
        if not GATE_AFTER:
            for part in range(2):
                x_copy(peer, me, part).wait_send()
        z_copy(peer, me).wait_send()
    for off in range(pack_size):
        peer = lax.rem(me + off, pack_size)
        pltpu.make_async_copy(finished.at[peer], out.at[peer], store.at[peer]).wait()

    @pl.when(slab < ctx_size - 1)
    def _():
        @pl.loop(0, chunks)
        def _(c):
            s_copy(c).wait_send()


def fused_body(
    signals, state_io, step_raw, row_target, table_start, log_rate, step_bias, skip_gain, norm_gain
):
    pack_size = lax.axis_size("pack")
    ctx_size = lax.axis_size("ctx")
    tokens = signals.shape[0]
    inner = signals.shape[1] // 2
    width = state_io.shape[1]
    state = width // 2
    head_count = log_rate.shape[0]
    block = tokens // pack_size
    chunks = inner // CHUNK
    vmem = pl.BlockSpec(memory_space=pltpu.VMEM)
    hbm = pl.BlockSpec(memory_space=pltpu.HBM)
    unsorted, order = pl.pallas_call(
        functools.partial(fused_kernel, pack_size, ctx_size, inner // head_count),
        out_shape=(
            jax.ShapeDtypeStruct((pack_size, block, inner), jnp.bfloat16),
            jax.ShapeDtypeStruct((tokens, tokens), jnp.bfloat16),
        ),
        in_specs=[hbm] * 9,
        out_specs=(hbm, vmem),
        scratch_shapes=[
            pltpu.VMEM((tokens, inner), jnp.bfloat16),
            pltpu.VMEM((tokens, inner), jnp.bfloat16),
            pltpu.VMEM((tokens, width), jnp.bfloat16),
            pltpu.VMEM((head_count, tokens), jnp.bfloat16),
            pltpu.SMEM((tokens // ROW,), jnp.int32),
            pltpu.SMEM((1, 1), jnp.int32),
            pltpu.VMEM((1, head_count), jnp.float32),
            pltpu.VMEM((1, head_count), jnp.float32),
            pltpu.VMEM((1, head_count), jnp.float32),
            pltpu.VMEM((1, inner), jnp.float32),
            pltpu.VMEM((2 * tokens + 16, 256), jnp.bfloat16),
            pltpu.VMEM((256, CHUNK), jnp.int32),
            pltpu.VMEM((tokens, width + 256), jnp.bfloat16),
            pltpu.VMEM((pack_size, block, inner + width + 256), jnp.bfloat16),
            pltpu.VMEM((pack_size, block, inner), jnp.bfloat16),
            pltpu.VMEM((pack_size, block, inner + width + 256), jnp.bfloat16),
            pltpu.VMEM((pack_size, block, inner), jnp.bfloat16),
            pltpu.VMEM((128, tokens), jnp.float32),
            pltpu.VMEM((pack_size, block, inner), jnp.float32),
            pltpu.VMEM((chunks, state, CHUNK), jnp.bfloat16),
            pltpu.VMEM((chunks, state, CHUNK), jnp.bfloat16),
            pltpu.VMEM((pack_size, block, inner), jnp.bfloat16),
            pltpu.SemaphoreType.DMA((10,)),
            pltpu.SemaphoreType.DMA((pack_size,)),
            pltpu.SemaphoreType.DMA((2, pack_size)),
            pltpu.SemaphoreType.DMA((2, pack_size)),
            pltpu.SemaphoreType.DMA((pack_size,)),
            pltpu.SemaphoreType.DMA((pack_size,)),
            pltpu.SemaphoreType.DMA((chunks,)),
            pltpu.SemaphoreType.DMA((chunks,)),
        ],
        compiler_params=pltpu.CompilerParams(
            collective_id=0, has_side_effects=True, vmem_limit_bytes=60 * 1024 * 1024
        ),
    )(
        signals,
        state_io,
        step_raw.T,
        row_target.reshape(-1),
        table_start,
        log_rate.reshape(1, -1),
        step_bias.reshape(1, -1),
        skip_gain.reshape(1, -1),
        norm_gain.reshape(1, -1),
    )
    return exact_permute(order, unsorted.reshape(tokens, inner))


def either_body(*arguments):
    one_group = arguments[0].shape[0] == GROUP and arguments[0].shape[1] % (2 * CHUNK) == 0
    return (fused_body if one_group else body)(*arguments)


def solution(mesh):
    return jax.shard_map(
        either_body,
        mesh=mesh,
        in_specs=(
            P(("pack", "ctx"), None),
            P(("pack", "ctx"), None),
            P(("pack", "ctx"), None),
            P("pack", "ctx", None),
            P("pack", "ctx"),
            P(),
            P(),
            P(),
            P(),
        ),
        out_specs=P(("pack", "ctx"), None),
        check_vma=False,
    )
```
